32 devices in a mesh: row: 16 (over z, y, core), col: 2 (over x).
Axes of the slice: x: 2, y: 2, z: 4, core: 2. Of those that a mesh axis runs over, the one named last changes fastest.
Arguments:
- row_embed: bfloat16 [300, 16384], P(None, 'row'), may hold values from -1.796875 to 1.796875
- col_embed: bfloat16 [300, 2, 256], P(None, 'col', 'row'), may hold values from -1.796875 to 1.796875
- counts: int32 [16384, 2, 256], P('row', 'col'), may hold values from 0 to 64, as said below
- occupancy: int32 [128, 2, 2], P('row', 'col'), may hold values from 0 to 1, as said below
- row_marg: int32 [16384], P('row'), may hold values from 2000 to 199999
- col_marg: int32 [2, 256], P('col', 'row'), may hold values from 2000 to 199999
- log_total: float32 [1], replicated, may hold values from 18 to 22
Outputs:
- grad_rows: float32 [300, 16384], P(None, 'row')
- grad_cols: float32 [300, 2, 256], P(None, 'col', 'row')
The draws below stay inside these ranges and needn't reach their ends.
Inputs may be any that keep to these rules, and one draw needn't show every extreme that they name: counts of the band's cells; zero in part of the cells. `occupancy`: the share of tiles marked 1 differs from row tile to row tile.
All inputs are finite; a program needn't handle non-finite values.
Results may differ from the reference program's by a relative error of at most 0.0018.
Values may be sent and summed in bfloat16 or wider, within the bound.
A program may use at most 64 MiB of HBM per device.

```python
import math
import jax
import jax.numpy as jnp
from jax import lax

D = 300
TILE = 128
ROW_DEV = 1024
ROWS = 16384
BAND = 256
BANDS = 2
COLS = 512
ROW_TILES = 128
BAND_TILES = 2


def draw_counts(key, part):
    present = jax.random.randint(jax.random.fold_in(key, 11), (ROWS, BANDS, BAND), 0, 2)
    values = jax.random.randint(jax.random.fold_in(key, 12), (ROWS, BANDS, BAND), 1, 65)
    result = (present * values).astype(jnp.int32)
    return result.at[0, 0, 0].set(64)


def draw_occupancy(key, part):
    levels = jax.random.randint(jax.random.fold_in(key, 21), (ROW_TILES, 1, 1), 1, 9)
    rolls = jax.random.randint(jax.random.fold_in(key, 22), (ROW_TILES, BANDS, BAND_TILES), 0, 8)
    return (rolls < levels).astype(jnp.int32)


def with_ends(values, rng, smallest, high):
    longest = values.shape.index(max(values.shape))
    spots = []
    for shift in (0, 1):
        where = [jax.random.randint(jax.random.fold_in(rng, axis), (), 0, length) for axis, length in enumerate(values.shape)]
        where[longest] = (where[longest] + shift) % values.shape[longest]
        spots.append(tuple(where))
    return values.at[spots[0]].set(smallest).at[spots[1]].set(high)


def block_scale(own_key, extent, shards, smallest, high):
    gain = 1.0
    for axis_at, blocks in shards:
        draws = jax.random.uniform(jax.random.fold_in(jax.random.fold_in(own_key, 6), axis_at), (blocks,), jnp.float32, smallest / len(shards), high / len(shards))
        gain = gain * jnp.repeat(jnp.exp(draws), extent[axis_at] // blocks).reshape((-1,) + (1,) * (len(extent) - 1 - axis_at))
    return gain


def normal_values(stream_key, extent, spread, most, shards=(), held_as=jnp.bfloat16):
    values = spread * jax.random.normal(stream_key, extent, jnp.float32)
    if shards:
        values = values * block_scale(stream_key, extent, shards, -0.22, 0.18)
    return jnp.clip(values, -most, most).astype(held_as)


def setup_inputs(seed: int = 0) -> dict:
    seeds = jax.random.split(jax.random.key(seed), 8)
    return {
        "row_embed": normal_values(seeds[0], (D, ROWS), 0.3, 1.796875, ((1, 16),)),
        "col_embed": normal_values(seeds[1], (D, BANDS, BAND), 0.3, 1.796875, ((1, 2), (2, 16))),
        "counts": draw_counts(jax.random.fold_in(seeds[7], 71), 0),
        "occupancy": draw_occupancy(jax.random.fold_in(seeds[7], 71), 0),
        "row_marg": with_ends(jax.random.randint(seeds[4], (ROWS,), 2000, 200000), jax.random.fold_in(seeds[4], 1), 2000, 199999).astype(jnp.int32),
        "col_marg": with_ends(jax.random.randint(seeds[5], (BANDS, BAND), 2000, 200000), jax.random.fold_in(seeds[5], 1), 2000, 199999).astype(jnp.int32),
        "log_total": jnp.clip(jax.random.uniform(seeds[6], (1,), jnp.float32, 18.0, 22.0), 18.0, 22.0),
    }


def cell_slope(scores, count_part, log_row_part, log_col_all, log_base):
    count_values = count_part.astype(jnp.float32)
    log_ratio = jnp.log(jnp.maximum(count_values, 1.0)) + (log_base - log_row_part[:, None] - log_col_all[None, :])
    score_gap = scores - log_ratio
    return jnp.where(count_part > 0, (0.1 + 0.25 * jnp.sqrt(count_values)) * score_gap, jax.nn.sigmoid(score_gap))

def reference(row_embed, col_embed, counts, occupancy, row_marg, col_marg, log_total):
    col_matrix = col_embed.reshape(D, COLS)
    count_matrix = counts.reshape(ROWS, COLS)
    occ_matrix = occupancy.reshape(ROW_TILES, COLS // TILE).astype(jnp.float32)
    log_col_all = jnp.log(col_marg.reshape(COLS).astype(jnp.float32))
    log_row = jnp.log(row_marg.astype(jnp.float32))
    log_base = log_total[0]
    block_tiles = ROW_DEV // TILE

    def row_block(col_total, block_index):
        first_row = (block_index * ROW_DEV).astype(jnp.int32)
        row_part = lax.dynamic_slice_in_dim(row_embed, first_row, ROW_DEV, 1)
        count_part = lax.dynamic_slice_in_dim(count_matrix, first_row, ROW_DEV, 0)
        log_row_part = lax.dynamic_slice_in_dim(log_row, first_row, ROW_DEV, 0)
        occ_part = lax.dynamic_slice_in_dim(occ_matrix, (block_index * block_tiles).astype(jnp.int32), block_tiles, 0)
        scores = jnp.dot(row_part.T, col_matrix, preferred_element_type=jnp.float32)
        slopes = cell_slope(scores, count_part, log_row_part, log_col_all, log_base)
        masked = slopes.reshape(block_tiles, TILE, COLS // TILE, TILE) * occ_part[:, None, :, None]
        residual = masked.reshape(ROW_DEV, COLS).astype(jnp.bfloat16)
        row_grads = jnp.dot(col_matrix, residual.T, preferred_element_type=jnp.float32)
        col_total = col_total + jnp.dot(row_part, residual, preferred_element_type=jnp.float32)
        return (col_total, row_grads)
    col_total, row_grads = lax.scan(row_block, jnp.zeros((D, COLS), jnp.float32), jnp.arange(ROWS // ROW_DEV, dtype=jnp.int32))
    grad_rows = row_grads.transpose(1, 0, 2).reshape(D, ROWS) * (1.0 / math.sqrt(COLS))
    grad_cols = (col_total * (1.0 / math.sqrt(ROWS))).reshape(D, BANDS, BAND)
    return (grad_rows, grad_cols)
```

```python
import functools
import math

import jax
import jax.numpy as jnp
from jax import lax
from jax.experimental import pallas as pl
from jax.experimental.pallas import tpu as pltpu
from jax.sharding import PartitionSpec as P

LANES = 128
SEND = jnp.bfloat16


def nt(a, b):
    return lax.dot_general(a, b, (((1,), (1,)), ((), ())), preferred_element_type=jnp.float32)


def nn(a, b):
    return lax.dot_general(a, b, (((1,), (0,)), ((), ())), preferred_element_type=jnp.float32)


def split3(x):
    hi = x.astype(jnp.bfloat16).astype(jnp.float32)
    rest = x - hi
    mid = rest.astype(jnp.bfloat16).astype(jnp.float32)
    return hi, mid, rest - mid


def eye(n):
    r = lax.broadcasted_iota(jnp.int32, (n, n), 0)
    c = lax.broadcasted_iota(jnp.int32, (n, n), 1)
    return (r == c).astype(jnp.float32).astype(jnp.bfloat16)


def slope_terms(code):
    slope = jnp.where(code > 0.0, 0.1 + 0.25 * jnp.sqrt(jnp.maximum(code, 0.0)), 0.0)
    return slope, jnp.log(jnp.maximum(code, 1.0))


def cell(code, slope, logc, gap):
    return jnp.where(code == 0.0, jax.nn.sigmoid(gap), slope * (gap - logc))


def repeat(n, fn):
    if n == 1:
        fn(0)
    else:
        pl.loop(0, n)(fn)


def kernel(cfg, r_hbm, c_ref, cnt_hbm, occ_ref, rm_ref, cm_ref, lt_ref,
           rows_out, cols_out,
           r_v, cnt_v, raug, blk, cg, cd, enc, slope_v, logc_v, res, gcol, s1buf, s2src, s2buf,
           dsem, gz_s, gz_r, gc_s, gc_r, gx_s, gx_r, e_s, e_r, a_s, a_r, b_s, b_r):
    n, d, dp, w, band, rows, tile, q_w, scale_r, scale_c = cfg
    half = n // 2
    nq = rows // q_w
    btiles = band // LANES
    sub = min(band, 256)
    nsub = band // sub
    me = lax.axis_index("row")
    col = lax.axis_index("col")
    core = lax.rem(me, 2)
    mate = me + 1 - 2 * core
    mine = me // 2
    peers = [lax.rem(me + 2 * k, n) for k in range(1, half)]
    froms = [lax.rem(me - 2 * k + n, n) for k in range(1, half)]
    at_mate = (mate, col)
    at_x = (me, 1 - col)

    def rcopy(src, dst, ss, rs, dev):
        return pltpu.make_async_remote_copy(
            src_ref=src, dst_ref=dst, send_sem=ss, recv_sem=rs,
            device_id=dev, device_id_type=pl.DeviceIdType.MESH)

    barrier = pltpu.get_barrier_semaphore()
    for dev in [(p, col) for p in peers] + [at_mate, at_x]:
        pl.semaphore_signal(barrier, inc=1, device_id=dev, device_id_type=pl.DeviceIdType.MESH)
    step = q_w * btiles
    loads = []
    for q in range(nq):
        cp = pltpu.make_async_copy(
            cnt_hbm.at[pl.ds(q * step, step), :], cnt_v.at[pl.ds(q * step, step), :], dsem.at[q])
        cp.start()
        loads.append(cp)
    rload = pltpu.make_async_copy(r_hbm, r_v, dsem.at[nq])
    rload.start()

    log_c = jnp.log(cm_ref[...].astype(jnp.float32))
    ri = lax.broadcasted_iota(jnp.int32, (w, w), 0)
    ci = lax.broadcasted_iota(jnp.int32, (w, w), 1)
    log_c = jnp.sum(jnp.where(ri == ci, jnp.broadcast_to(log_c, (w, w)), 0.0), axis=1, keepdims=True)
    hi, mid, lo = split3(log_c)
    blk[...] = jnp.zeros_like(blk)
    blk[:, pl.ds(0, d)] = c_ref[...].astype(jnp.float32)
    li = lax.broadcasted_iota(jnp.int32, (w, dp), 1)
    own = blk[...]
    for at, val in ((d, hi), (d + 1, mid), (d + 2, lo)):
        own = jnp.where(li == at, val, own)
    own = jnp.where((li >= d + 3) & (li < d + 6), 1.0, own)
    cg[0, me] = own.astype(jnp.bfloat16)

    ident = eye(LANES)

    def encode(q):
        loads[q].wait()

        def part(t):
            cells = []
            for u in range(q_w // tile):
                x = cnt_v[pl.ds(q * step + u * tile * btiles + t, tile, stride=btiles), :]
                on = occ_ref[t, q * (q_w // tile) + u] != 0
                cells.append(jnp.where(on, x, -1).astype(jnp.float32).astype(jnp.bfloat16))
            code = nt(ident, jnp.concatenate(cells, axis=0))
            at = pl.ds(t * LANES, LANES)
            enc[0, q, at, :] = code.astype(jnp.bfloat16)
            slope_v[q, at, :], logc_v[q, at, :] = slope_terms(code)

        for t in range(btiles):
            part(t)

    encode(0)
    pl.semaphore_wait(barrier, half + 1)

    xcp = rcopy(cg.at[0, me], cg.at[1, me], gx_s, gx_r, at_x)
    xcp.start()
    sends = [xcp]
    for p in peers:
        cp = rcopy(cg.at[0, me], cg.at[0, me], gz_s.at[0, p // 2], gz_r.at[0, mine], (p, col))
        cp.start()
        sends.append(cp)
    cp = rcopy(cg.at[0, me], cg.at[0, me], gc_s.at[0, mine], gc_r.at[0, mine], at_mate)
    cp.start()
    sends.append(cp)

    ecopies = [rcopy(enc.at[0, q], enc.at[1, q], e_s.at[q], e_r.at[q], at_x) for q in range(nq)]
    for q in range(1, nq):
        ecopies[q - 1].start()
        encode(q)

    rload.wait()
    raug[pl.ds(0, d), :] = r_v[...]
    first = (d // 16) * 16
    row_term = jnp.log(rm_ref[...].astype(jnp.float32)) - lt_ref[0]
    hi, mid, lo = split3(row_term)
    tail = raug[pl.ds(first, dp - first), :].astype(jnp.float32)
    si = lax.broadcasted_iota(jnp.int32, (dp - first, rows), 0) + first
    tail = jnp.where(si < d, tail, jnp.where(si < d + 3, 1.0, 0.0))
    for at, val in ((d + 3, hi), (d + 4, mid), (d + 5, lo)):
        tail = jnp.where(si == at, val, tail)
    raug[pl.ds(first, dp - first), :] = tail.astype(jnp.bfloat16)
    ecopies[nq - 1].start()

    xcp.wait_recv()
    for p in peers:
        cp = rcopy(cg.at[1, me], cg.at[1, me], gz_s.at[1, p // 2], gz_r.at[1, mine], (p, col))
        cp.start()
        sends.append(cp)
    cp = rcopy(cg.at[1, me], cg.at[1, me], gc_s.at[1, mine], gc_r.at[1, mine], at_mate)
    cp.start()
    sends.append(cp)

    def forward(which):
        for p in froms:
            rcopy(cg.at[which, p], cg.at[which, p], gz_s.at[which, p // 2],
                  gz_r.at[which, p // 2], at_mate).wait_recv()
            cp = rcopy(cg.at[which, p], cg.at[which, p], gc_s.at[which, p // 2],
                       gc_r.at[which, p // 2], at_mate)
            cp.start()
            sends.append(cp)

    def mate_blocks(which):
        for k in range(half):
            at = 2 * k + 1 - core
            rcopy(cg.at[which, at], cg.at[which, at], gc_s.at[which, k],
                  gc_r.at[which, k], at_mate).wait_recv()

    forward(0)
    mate_blocks(0)

    per = sub // w

    def block(which, s):
        return cg[which, pl.ds(s * per, per)].reshape(sub, dp)

    for q in range(nq):
        qs = pl.ds(q * q_w, q_w)

        def cells(s):
            at = pl.ds(s * sub, sub)
            gap = nn(block(0, s), raug[:, qs])
            code = enc[0, q, at, :].astype(jnp.float32)
            res[at, qs] = cell(code, slope_v[q, at, :], logc_v[q, at, :], gap).astype(jnp.bfloat16)

        repeat(nsub, cells)

    def col_terms(s):
        gcol[pl.ds(s * per, per)] = nt(res[pl.ds(s * sub, sub), :], raug[...]).reshape(per, w, dp)

    repeat(nsub, col_terms)
    for k in range(half):
        cp = rcopy(gcol.at[2 * k + 1 - core], s1buf.at[k], a_s.at[k], a_r.at[k], at_mate)
        cp.start()
        sends.append(cp)

    ident_d = eye(dp)

    def transposed(which):
        def one(s):
            cd[which, :, pl.ds(s * sub, sub)] = nt(ident_d, block(which, s)).astype(jnp.bfloat16)

        repeat(nsub, one)

    transposed(0)
    rows_out[...] = nn(cd[0], res[...])[:d, :]

    forward(1)
    for k in range(half):
        rcopy(gcol.at[k], s1buf.at[k], a_s.at[k], a_r.at[k], at_mate).wait_recv()
    for p in peers:
        s2src[p // 2] = (gcol[p] + s1buf[p // 2]).astype(s2src.dtype)
    total = gcol[me] + s1buf[mine]
    mate_blocks(1)
    for p in peers:
        cp = rcopy(s2src.at[p // 2], s2buf.at[mine], b_s.at[p // 2], b_r.at[mine], (p, col))
        cp.start()
        sends.append(cp)

    transposed(1)
    for q in range(nq):
        qs = pl.ds(q * q_w, q_w)
        ecopies[q].wait_recv()

        def cells(s):
            at = pl.ds(s * sub, sub)
            gap = nn(block(1, s), raug[:, qs])
            code = enc[1, q, at, :].astype(jnp.float32)
            slope, logc = slope_terms(code)
            res[at, qs] = cell(code, slope, logc, gap).astype(jnp.bfloat16)

        repeat(nsub, cells)
        rows_out[:, qs] = (rows_out[:, qs] + nn(cd[1], res[:, qs])[:d, :]) * scale_r

    for p in froms:
        rcopy(s2src.at[0], s2buf.at[p // 2], b_s.at[p // 2], b_r.at[p // 2], at_mate).wait_recv()
        total = total + s2buf[p // 2].astype(jnp.float32)
    cols_out[...] = (total * scale_c)[:, :d]
    for cp in sends + ecopies:
        cp.wait_send()


def body(row_embed, col_embed, counts, occupancy, row_marg, col_marg, log_total):
    n = lax.axis_size("row")
    d, rows = row_embed.shape
    w = col_embed.shape[2]
    band = counts.shape[2]
    tile = rows // occupancy.shape[0]
    q_w = 2 * tile if rows % (2 * tile) == 0 else tile
    dp = -(-(d + 6) // LANES) * LANES
    half = n // 2
    nq = rows // q_w
    btiles = band // LANES
    cfg = (n, d, dp, w, band, rows, tile, q_w,
           1.0 / math.sqrt(w * n * lax.axis_size("col")), 1.0 / math.sqrt(rows * n))
    bf, f32 = jnp.bfloat16, jnp.float32
    vm, sm, hb = (pl.BlockSpec(memory_space=m) for m in (pltpu.VMEM, pltpu.SMEM, pl.ANY))
    dma = lambda *s: pltpu.SemaphoreType.DMA(s) if s else pltpu.SemaphoreType.DMA
    grad_rows, grad_cols = pl.pallas_call(
        functools.partial(kernel, cfg),
        out_shape=(jax.ShapeDtypeStruct((d, rows), f32), jax.ShapeDtypeStruct((w, d), f32)),
        in_specs=[hb, vm, hb, sm, vm, vm, sm],
        out_specs=(vm, vm),
        scratch_shapes=[
            pltpu.VMEM((d, rows), bf),
            pltpu.VMEM((rows * btiles, LANES), jnp.int32),
            pltpu.VMEM((dp, rows), bf),
            pltpu.VMEM((w, dp), f32),
            pltpu.VMEM((2, n, w, dp), bf),
            pltpu.VMEM((2, dp, band), bf),
            pltpu.VMEM((2, nq, band, q_w), bf),
            pltpu.VMEM((nq, band, q_w), f32),
            pltpu.VMEM((nq, band, q_w), f32),
            pltpu.VMEM((band, rows), bf),
            pltpu.VMEM((n, w, dp), f32),
            pltpu.VMEM((half, w, dp), f32),
            pltpu.VMEM((half, w, dp), SEND),
            pltpu.VMEM((half, w, dp), SEND),
            dma(nq + 1),
            dma(2, half), dma(2, half), dma(2, half), dma(2, half), dma(), dma(),
            dma(nq), dma(nq), dma(half), dma(half), dma(half), dma(half),
        ],
        compiler_params=pltpu.CompilerParams(
            collective_id=0, has_side_effects=True, vmem_limit_bytes=60 * 1024 * 1024),
    )(
        row_embed,
        jnp.transpose(col_embed, (1, 2, 0)).reshape(w, d),
        counts.reshape(rows * btiles, LANES),
        jnp.transpose(occupancy, (1, 2, 0)).reshape(occupancy.shape[2], occupancy.shape[0]),
        row_marg.reshape(1, rows),
        col_marg,
        log_total,
    )
    return grad_rows, jnp.transpose(grad_cols.reshape(1, w, d), (2, 0, 1))


def solution(mesh):
    placed = (
        P(None, "row"),
        P(None, "col", "row"),
        P("row", "col", None),
        P("row", "col", None),
        P("row"),
        P("col", "row"),
        P(),
    )
    return jax.shard_map(
        body,
        mesh=mesh,
        in_specs=placed,
        out_specs=(P(None, "row"), P(None, "col", "row")),
        check_vma=False,
    )
```

```python
import functools
import math

import jax
import jax.numpy as jnp
from jax import lax
from jax.experimental import pallas as pl
from jax.experimental.pallas import tpu as pltpu
from jax.sharding import PartitionSpec as P

LANES = 128
SEND = jnp.bfloat16


def nt(a, b):
    return lax.dot_general(a, b, (((1,), (1,)), ((), ())), preferred_element_type=jnp.float32)


def nn(a, b):
    return lax.dot_general(a, b, (((1,), (0,)), ((), ())), preferred_element_type=jnp.float32)


def split3(x):
    hi = x.astype(jnp.bfloat16).astype(jnp.float32)
    rest = x - hi
    mid = rest.astype(jnp.bfloat16).astype(jnp.float32)
    return hi, mid, rest - mid


def eye(n):
    r = lax.broadcasted_iota(jnp.int32, (n, n), 0)
    c = lax.broadcasted_iota(jnp.int32, (n, n), 1)
    return (r == c).astype(jnp.float32).astype(jnp.bfloat16)


def slope_terms(code):
    slope = jnp.where(code > 0.0, 0.1 + 0.25 * jnp.sqrt(jnp.maximum(code, 0.0)), 0.0)
    return slope, jnp.log(jnp.maximum(code, 1.0))


def cell(code, slope, logc, gap):
    return jnp.where(code == 0.0, jax.nn.sigmoid(gap), slope * (gap - logc))


def repeat(n, fn):
    if n == 1:
        fn(0)
    else:
        pl.loop(0, n)(fn)


def kernel(cfg, r_hbm, c_hbm, cnt_hbm, occ_hbm, rm_hbm, cm_hbm, lt_ref,
           rows_out, cols_out,
           r_v, cnt_v, raug, blk, cg, cd, enc, slope_v, logc_v, res, gcol, s1buf, s2src, s2buf,
           c_ref, occ_ref, rm_ref, cm_ref, dsem, gz_s, gz_r, gc_s, gc_r, gx_s, gx_r, e_s, e_r, a_s, a_r, b_s, b_r):
    n, d, dp, w, band, rows, tile, q_w, scale_r, scale_c = cfg
    half = n // 2
    nq = rows // q_w
    btiles = band // LANES
    sub = min(band, 256)
    nsub = band // sub
    me = lax.axis_index("row")
    col = lax.axis_index("col")
    core = lax.rem(me, 2)
    mate = me + 1 - 2 * core
    mine = me // 2
    peers = [lax.rem(me + 2 * k, n) for k in range(1, half)]
    froms = [lax.rem(me - 2 * k + n, n) for k in range(1, half)]
    at_mate = (mate, col)
    at_x = (me, 1 - col)

    def rcopy(src, dst, ss, rs, dev):
        return pltpu.make_async_remote_copy(
            src_ref=src, dst_ref=dst, send_sem=ss, recv_sem=rs,
            device_id=dev, device_id_type=pl.DeviceIdType.MESH)

    barrier = pltpu.get_barrier_semaphore()
    for dev in [(p, col) for p in peers] + [at_mate, at_x]:
        pl.semaphore_signal(barrier, inc=1, device_id=dev, device_id_type=pl.DeviceIdType.MESH)
    small = []
    for k, (src, dst) in enumerate(((cm_hbm, cm_ref), (c_hbm, c_ref), (occ_hbm, occ_ref),
                                    (rm_hbm, rm_ref))):
        cp = pltpu.make_async_copy(src, dst, dsem.at[nq + 1 + k])
        cp.start()
        small.append(cp)
    step = q_w * btiles
    loads = []
    for q in range(nq):
        cp = pltpu.make_async_copy(
            cnt_hbm.at[pl.ds(q * step, step), :], cnt_v.at[pl.ds(q * step, step), :], dsem.at[q])
        cp.start()
        loads.append(cp)
    rload = pltpu.make_async_copy(r_hbm, r_v, dsem.at[nq])
    rload.start()

    for cp in small:
        cp.wait()

    log_c = jnp.log(cm_ref[...].astype(jnp.float32))
    ri = lax.broadcasted_iota(jnp.int32, (w, w), 0)
    ci = lax.broadcasted_iota(jnp.int32, (w, w), 1)
    log_c = jnp.sum(jnp.where(ri == ci, jnp.broadcast_to(log_c, (w, w)), 0.0), axis=1, keepdims=True)
    hi, mid, lo = split3(log_c)
    blk[...] = jnp.zeros_like(blk)
    blk[:, pl.ds(0, d)] = c_ref[...].astype(jnp.float32)
    li = lax.broadcasted_iota(jnp.int32, (w, dp), 1)
    own = blk[...]
    for at, val in ((d, hi), (d + 1, mid), (d + 2, lo)):
        own = jnp.where(li == at, val, own)
    own = jnp.where((li >= d + 3) & (li < d + 6), 1.0, own)
    cg[0, me] = own.astype(jnp.bfloat16)

    ident = eye(LANES)

    def encode(q):
        loads[q].wait()

        def part(t):
            cells = []
            for u in range(q_w // tile):
                x = cnt_v[pl.ds(q * step + u * tile * btiles + t, tile, stride=btiles), :]
                k = q * (q_w // tile) + u
                on = jnp.broadcast_to(occ_ref[t:t + 1, k:k + 1], (tile, LANES)) != 0
                cells.append(jnp.where(on, x, -1).astype(jnp.float32).astype(jnp.bfloat16))
            code = nt(ident, jnp.concatenate(cells, axis=0))
            at = pl.ds(t * LANES, LANES)
            enc[0, q, at, :] = code.astype(jnp.bfloat16)
            slope_v[q, at, :], logc_v[q, at, :] = slope_terms(code)

        for t in range(btiles):
            part(t)

    encode(0)
    pl.semaphore_wait(barrier, half + 1)

    xcp = rcopy(cg.at[0, me], cg.at[1, me], gx_s, gx_r, at_x)
    xcp.start()
    sends = [xcp]
    for p in peers:
        cp = rcopy(cg.at[0, me], cg.at[0, me], gz_s.at[0, p // 2], gz_r.at[0, mine], (p, col))
        cp.start()
        sends.append(cp)
    cp = rcopy(cg.at[0, me], cg.at[0, me], gc_s.at[0, mine], gc_r.at[0, mine], at_mate)
    cp.start()
    sends.append(cp)

    ecopies = [rcopy(enc.at[0, q], enc.at[1, q], e_s.at[q], e_r.at[q], at_x) for q in range(nq)]
    for q in range(1, nq):
        ecopies[q - 1].start()
        encode(q)

    rload.wait()
    raug[pl.ds(0, d), :] = r_v[...]
    first = (d // 16) * 16
    row_term = jnp.log(rm_ref[...].astype(jnp.float32)) - lt_ref[0]
    hi, mid, lo = split3(row_term)
    tail = raug[pl.ds(first, dp - first), :].astype(jnp.float32)
    si = lax.broadcasted_iota(jnp.int32, (dp - first, rows), 0) + first
    tail = jnp.where(si < d, tail, jnp.where(si < d + 3, 1.0, 0.0))
    for at, val in ((d + 3, hi), (d + 4, mid), (d + 5, lo)):
        tail = jnp.where(si == at, val, tail)
    raug[pl.ds(first, dp - first), :] = tail.astype(jnp.bfloat16)
    ecopies[nq - 1].start()

    xcp.wait_recv()
    for p in peers:
        cp = rcopy(cg.at[1, me], cg.at[1, me], gz_s.at[1, p // 2], gz_r.at[1, mine], (p, col))
        cp.start()
        sends.append(cp)
    cp = rcopy(cg.at[1, me], cg.at[1, me], gc_s.at[1, mine], gc_r.at[1, mine], at_mate)
    cp.start()
    sends.append(cp)

    def forward(which):
        for p in froms:
            rcopy(cg.at[which, p], cg.at[which, p], gz_s.at[which, p // 2],
                  gz_r.at[which, p // 2], at_mate).wait_recv()
            cp = rcopy(cg.at[which, p], cg.at[which, p], gc_s.at[which, p // 2],
                       gc_r.at[which, p // 2], at_mate)
            cp.start()
            sends.append(cp)

    def mate_blocks(which):
        for k in range(half):
            at = 2 * k + 1 - core
            rcopy(cg.at[which, at], cg.at[which, at], gc_s.at[which, k],
                  gc_r.at[which, k], at_mate).wait_recv()

    forward(0)
    mate_blocks(0)

    per = sub // w

    def block(which, s):
        return cg[which, pl.ds(s * per, per)].reshape(sub, dp)

    for q in range(nq):
        qs = pl.ds(q * q_w, q_w)

        def cells(s):
            at = pl.ds(s * sub, sub)
            gap = nn(block(0, s), raug[:, qs])
            code = enc[0, q, at, :].astype(jnp.float32)
            res[at, qs] = cell(code, slope_v[q, at, :], logc_v[q, at, :], gap).astype(jnp.bfloat16)

        repeat(nsub, cells)

    def col_terms(s):
        gcol[pl.ds(s * per, per)] = nt(res[pl.ds(s * sub, sub), :], raug[...]).reshape(per, w, dp)

    repeat(nsub, col_terms)
    for k in range(half):
        cp = rcopy(gcol.at[2 * k + 1 - core], s1buf.at[k], a_s.at[k], a_r.at[k], at_mate)
        cp.start()
        sends.append(cp)

    ident_d = eye(dp)

    def transposed(which):
        def one(s):
            cd[which, :, pl.ds(s * sub, sub)] = nt(ident_d, block(which, s)).astype(jnp.bfloat16)

        repeat(nsub, one)

    transposed(0)
    rows_out[...] = nn(cd[0], res[...])[:d, :]

    forward(1)
    for k in range(half):
        rcopy(gcol.at[k], s1buf.at[k], a_s.at[k], a_r.at[k], at_mate).wait_recv()
    for p in peers:
        s2src[p // 2] = (gcol[p] + s1buf[p // 2]).astype(s2src.dtype)
    total = gcol[me] + s1buf[mine]
    mate_blocks(1)
    for p in peers:
        cp = rcopy(s2src.at[p // 2], s2buf.at[mine], b_s.at[p // 2], b_r.at[mine], (p, col))
        cp.start()
        sends.append(cp)

    transposed(1)
    for q in range(nq):
        qs = pl.ds(q * q_w, q_w)
        ecopies[q].wait_recv()

        def cells(s):
            at = pl.ds(s * sub, sub)
            gap = nn(block(1, s), raug[:, qs])
            code = enc[1, q, at, :].astype(jnp.float32)
            slope, logc = slope_terms(code)
            res[at, qs] = cell(code, slope, logc, gap).astype(jnp.bfloat16)

        repeat(nsub, cells)
        rows_out[:, qs] = (rows_out[:, qs] + nn(cd[1], res[:, qs])[:d, :]) * scale_r

    for p in froms:
        rcopy(s2src.at[0], s2buf.at[p // 2], b_s.at[p // 2], b_r.at[p // 2], at_mate).wait_recv()
        total = total + s2buf[p // 2].astype(jnp.float32)
    cols_out[...] = (total * scale_c)[:, :d]
    for cp in sends + ecopies:
        cp.wait_send()


def scratch_bytes(shapes):
    return sum(math.prod(s.shape) * jnp.dtype(s.dtype).itemsize for s in shapes)


def place(rows_in, cols_in, rows_out, cols_out, sem):
    copies = [pltpu.make_async_copy(rows_in, rows_out, sem.at[0]),
              pltpu.make_async_copy(cols_in, cols_out, sem.at[1])]
    for cp in copies:
        cp.start()
    for cp in copies:
        cp.wait()


def body(row_embed, col_embed, counts, occupancy, row_marg, col_marg, log_total):
    n = lax.axis_size("row")
    d, rows = row_embed.shape
    w = col_embed.shape[2]
    band = counts.shape[2]
    tile = rows // occupancy.shape[0]
    q_w = 2 * tile if rows % (2 * tile) == 0 else tile
    dp = -(-(d + 6) // LANES) * LANES
    half = n // 2
    nq = rows // q_w
    btiles = band // LANES
    cfg = (n, d, dp, w, band, rows, tile, q_w,
           1.0 / math.sqrt(w * n * lax.axis_size("col")), 1.0 / math.sqrt(rows * n))
    bf, f32 = jnp.bfloat16, jnp.float32
    vm, hb, anywhere = (pl.BlockSpec(memory_space=m) for m in (pltpu.VMEM, pltpu.HBM, pl.ANY))
    dma = lambda *s: pltpu.SemaphoreType.DMA(s) if s else pltpu.SemaphoreType.DMA
    scratch = [
        pltpu.VMEM((d, rows), bf),
        pltpu.VMEM((rows * btiles, LANES), jnp.int32),
        pltpu.VMEM((dp, rows), bf),
        pltpu.VMEM((w, dp), f32),
        pltpu.VMEM((2, n, w, dp), bf),
        pltpu.VMEM((2, dp, band), bf),
        pltpu.VMEM((2, nq, band, q_w), bf),
        pltpu.VMEM((nq, band, q_w), f32),
        pltpu.VMEM((nq, band, q_w), f32),
        pltpu.VMEM((band, rows), bf),
        pltpu.VMEM((n, w, dp), f32),
        pltpu.VMEM((half, w, dp), f32),
        pltpu.VMEM((half, w, dp), SEND),
        pltpu.VMEM((half, w, dp), SEND),
        pltpu.VMEM((w, d), bf),
        pltpu.VMEM((occupancy.shape[2], occupancy.shape[0]), jnp.int32),
        pltpu.VMEM((1, rows), jnp.int32),
        pltpu.VMEM((1, w), jnp.int32),
        dma(nq + 5),
        dma(2, half), dma(2, half), dma(2, half), dma(2, half), dma(), dma(),
        dma(nq), dma(nq), dma(half), dma(half), dma(half), dma(half),
    ]
    limit = min(60 << 20, (6 << 20) + scratch_bytes(scratch[:18]) + 2 * d * rows * 4 + 24 * band * q_w)
    grad_rows, grad_cols = pl.pallas_call(
        functools.partial(kernel, cfg),
        out_shape=(jax.ShapeDtypeStruct((d, rows), f32), jax.ShapeDtypeStruct((w, d), f32)),
        in_specs=[hb] * 6 + [pl.BlockSpec(memory_space=pltpu.SMEM)],
        out_specs=(vm, vm),
        scratch_shapes=scratch,
        compiler_params=pltpu.CompilerParams(
            collective_id=0, has_side_effects=True, vmem_limit_bytes=limit),
    )(
        *(pltpu.with_memory_space_constraint(x, pltpu.HBM) for x in (
            row_embed,
            jnp.transpose(col_embed, (1, 2, 0)).reshape(w, d),
            counts.reshape(rows * btiles, LANES),
            jnp.transpose(occupancy, (1, 2, 0)).reshape(occupancy.shape[2], occupancy.shape[0]),
            row_marg.reshape(1, rows),
            col_marg,
        )),
        log_total,
    )
    grad_rows, grad_cols = pl.pallas_call(
        place,
        out_shape=(jax.ShapeDtypeStruct((d, rows), f32), jax.ShapeDtypeStruct((w, d), f32)),
        in_specs=[anywhere, anywhere],
        out_specs=(hb, hb),
        scratch_shapes=[pltpu.SemaphoreType.DMA((2,))],
    )(*(pltpu.with_memory_space_constraint(x, pltpu.VMEM) for x in (grad_rows, grad_cols)))
    return grad_rows, jnp.transpose(grad_cols.reshape(1, w, d), (2, 0, 1))


def solution(mesh):
    placed = (
        P(None, "row"),
        P(None, "col", "row"),
        P("row", "col", None),
        P("row", "col", None),
        P("row"),
        P("col", "row"),
        P(),
    )
    return jax.shard_map(
        body,
        mesh=mesh,
        in_specs=placed,
        out_specs=(P(None, "row"), P(None, "col", "row")),
        check_vma=False,
    )
```

```python
import functools
import math

import jax
import jax.numpy as jnp
from jax import lax
from jax.experimental import pallas as pl
from jax.experimental.pallas import tpu as pltpu
from jax.sharding import PartitionSpec as P

LANES = 128
SEND = jnp.bfloat16


def nt(a, b):
    return lax.dot_general(a, b, (((1,), (1,)), ((), ())), preferred_element_type=jnp.float32)


def nn(a, b):
    return lax.dot_general(a, b, (((1,), (0,)), ((), ())), preferred_element_type=jnp.float32)


def split3(x):
    hi = x.astype(jnp.bfloat16).astype(jnp.float32)
    rest = x - hi
    mid = rest.astype(jnp.bfloat16).astype(jnp.float32)
    return hi, mid, rest - mid


def eye(n):
    r = lax.broadcasted_iota(jnp.int32, (n, n), 0)
    c = lax.broadcasted_iota(jnp.int32, (n, n), 1)
    return (r == c).astype(jnp.float32).astype(jnp.bfloat16)


def slope_terms(code):
    slope = jnp.where(code > 0.0, 0.1 + 0.25 * jnp.sqrt(jnp.maximum(code, 0.0)), 0.0)
    return slope, jnp.log(jnp.maximum(code, 1.0))


def cell(code, slope, logc, gap):
    return jnp.where(code == 0.0, jax.nn.sigmoid(gap), slope * (gap - logc))


def repeat(n, fn):
    if n == 1:
        fn(0)
    else:
        pl.loop(0, n)(fn)


def kernel(cfg, r_hbm, c_hbm, cnt_hbm, occ_hbm, rm_hbm, cm_hbm, lt_ref,
           rows_out, cols_out,
           r_v, cnt_v, raug, blk, cg, cd, enc, slope_v, logc_v, res, gcol, s1buf, s2src, s2buf,
           c_ref, occ_ref, rm_ref, cm_ref, dsem, gz_s, gz_r, gc_s, gc_r, gx_s, gx_r, e_s, e_r, a_s, a_r, b_s, b_r, token):
    n, d, dp, w, band, rows, tile, q_w, scale_r, scale_c = cfg
    half = n // 2
    nq = rows // q_w
    btiles = band // LANES
    sub = min(band, 256)
    nsub = band // sub
    me = lax.axis_index("row")
    col = lax.axis_index("col")
    core = lax.rem(me, 2)
    mate = me + 1 - 2 * core
    mine = me // 2
    peers = [lax.rem(me + 2 * k, n) for k in range(1, half)]
    froms = [lax.rem(me - 2 * k + n, n) for k in range(1, half)]
    at_mate = (mate, col)
    at_x = (me, 1 - col)

    def rcopy(src, dst, ss, rs, dev):
        return pltpu.make_async_remote_copy(
            src_ref=src, dst_ref=dst, send_sem=ss, recv_sem=rs,
            device_id=dev, device_id_type=pl.DeviceIdType.MESH)

    barrier = pltpu.get_barrier_semaphore()
    masks = [half >> k for k in range(1, half.bit_length())]
    near = [(2 * (mine + m - 2 * m * lax.rem(mine // m, 2)) + core, col) for m in masks]
    for dev in near + [at_mate, at_x]:
        pl.semaphore_signal(barrier, inc=1, device_id=dev, device_id_type=pl.DeviceIdType.MESH)
    small = []
    for k, (src, dst) in enumerate(((cm_hbm, cm_ref), (c_hbm, c_ref), (occ_hbm, occ_ref),
                                    (rm_hbm, rm_ref))):
        cp = pltpu.make_async_copy(src, dst, dsem.at[nq + 1 + k])
        cp.start()
        small.append(cp)
    step = q_w * btiles
    loads = []
    for q in range(nq):
        cp = pltpu.make_async_copy(
            cnt_hbm.at[pl.ds(q * step, step), :], cnt_v.at[pl.ds(q * step, step), :], dsem.at[q])
        cp.start()
        loads.append(cp)
    rload = pltpu.make_async_copy(r_hbm, r_v, dsem.at[nq])
    rload.start()

    for cp in small:
        cp.wait()

    log_c = jnp.log(cm_ref[...].astype(jnp.float32))
    ri = lax.broadcasted_iota(jnp.int32, (w, w), 0)
    ci = lax.broadcasted_iota(jnp.int32, (w, w), 1)
    log_c = jnp.sum(jnp.where(ri == ci, jnp.broadcast_to(log_c, (w, w)), 0.0), axis=1, keepdims=True)
    hi, mid, lo = split3(log_c)
    blk[...] = jnp.zeros_like(blk)
    blk[:, pl.ds(0, d)] = c_ref[...].astype(jnp.float32)
    li = lax.broadcasted_iota(jnp.int32, (w, dp), 1)
    own = blk[...]
    for at, val in ((d, hi), (d + 1, mid), (d + 2, lo)):
        own = jnp.where(li == at, val, own)
    own = jnp.where((li >= d + 3) & (li < d + 6), 1.0, own)
    cg[0, me] = own.astype(jnp.bfloat16)

    ident = eye(LANES)

    def encode(q):
        loads[q].wait()

        def part(t):
            cells = []
            for u in range(q_w // tile):
                x = cnt_v[pl.ds(q * step + u * tile * btiles + t, tile, stride=btiles), :]
                k = q * (q_w // tile) + u
                on = jnp.broadcast_to(occ_ref[t:t + 1, k:k + 1], (tile, LANES)) != 0
                cells.append(jnp.where(on, x, -1).astype(jnp.float32).astype(jnp.bfloat16))
            code = nt(ident, jnp.concatenate(cells, axis=0))
            at = pl.ds(t * LANES, LANES)
            enc[0, q, at, :] = code.astype(jnp.bfloat16)
            slope_v[q, at, :], logc_v[q, at, :] = slope_terms(code)

        for t in range(btiles):
            part(t)

    ecopies = [rcopy(enc.at[0, q], enc.at[1, q], e_s.at[q], e_r.at[q], at_x) for q in range(nq)]
    encode(0)
    pl.semaphore_wait(barrier, len(masks) + 2)
    ecopies[0].start()
    xcp = rcopy(cg.at[0, me], cg.at[1, me], gx_s, gx_r, at_x)
    xcp.start()
    sends = [xcp]
    cp = rcopy(cg.at[0, me], cg.at[0, me], gc_s.at[0, mine], gc_r.at[0, mine], at_mate)
    cp.start()
    sends.append(cp)

    done = 1
    for k in range(1, len(masks)):
        pl.semaphore_signal(token.at[k], inc=1, device_id=near[k], device_id_type=pl.DeviceIdType.MESH)
        if done < nq:
            encode(done)
        pl.semaphore_wait(token.at[k], 1)
        if done < nq:
            ecopies[done].start()
            done += 1

    for p in peers:
        cp = rcopy(cg.at[0, me], cg.at[0, me], gz_s.at[0, p // 2], gz_r.at[0, mine], (p, col))
        cp.start()
        sends.append(cp)
    for q in range(done, nq):
        encode(q)
        if q > done:
            ecopies[q - 1].start()

    xcp.wait_recv()
    for p in peers:
        cp = rcopy(cg.at[1, me], cg.at[1, me], gz_s.at[1, p // 2], gz_r.at[1, mine], (p, col))
        cp.start()
        sends.append(cp)
    cp = rcopy(cg.at[1, me], cg.at[1, me], gc_s.at[1, mine], gc_r.at[1, mine], at_mate)
    cp.start()
    sends.append(cp)

    if done < nq:
        ecopies[nq - 1].start()

    rload.wait()
    raug[pl.ds(0, d), :] = r_v[...]
    first = (d // 16) * 16
    row_term = jnp.log(rm_ref[...].astype(jnp.float32)) - lt_ref[0]
    hi, mid, lo = split3(row_term)
    tail = raug[pl.ds(first, dp - first), :].astype(jnp.float32)
    si = lax.broadcasted_iota(jnp.int32, (dp - first, rows), 0) + first
    tail = jnp.where(si < d, tail, jnp.where(si < d + 3, 1.0, 0.0))
    for at, val in ((d + 3, hi), (d + 4, mid), (d + 5, lo)):
        tail = jnp.where(si == at, val, tail)
    raug[pl.ds(first, dp - first), :] = tail.astype(jnp.bfloat16)

    def forward(which):
        for p in froms:
            rcopy(cg.at[which, p], cg.at[which, p], gz_s.at[which, p // 2],
                  gz_r.at[which, p // 2], at_mate).wait_recv()
            cp = rcopy(cg.at[which, p], cg.at[which, p], gc_s.at[which, p // 2],
                       gc_r.at[which, p // 2], at_mate)
            cp.start()
            sends.append(cp)

    def mate_blocks(which):
        for k in range(half):
            at = 2 * k + 1 - core
            rcopy(cg.at[which, at], cg.at[which, at], gc_s.at[which, k],
                  gc_r.at[which, k], at_mate).wait_recv()

    forward(0)
    mate_blocks(0)

    per = sub // w

    def block(which, s):
        return cg[which, pl.ds(s * per, per)].reshape(sub, dp)

    for q in range(nq):
        qs = pl.ds(q * q_w, q_w)

        def cells(s):
            at = pl.ds(s * sub, sub)
            gap = nn(block(0, s), raug[:, qs])
            code = enc[0, q, at, :].astype(jnp.float32)
            res[at, qs] = cell(code, slope_v[q, at, :], logc_v[q, at, :], gap).astype(jnp.bfloat16)

        repeat(nsub, cells)

    def col_terms(s):
        gcol[pl.ds(s * per, per)] = nt(res[pl.ds(s * sub, sub), :], raug[...]).reshape(per, w, dp)

    repeat(nsub, col_terms)
    for p in peers + [me]:
        k = p // 2
        cp = rcopy(gcol.at[2 * k + 1 - core], s1buf.at[k], a_s.at[k], a_r.at[k], at_mate)
        cp.start()
        sends.append(cp)

    ident_d = eye(dp)

    def transposed(which):
        def one(s):
            cd[which, :, pl.ds(s * sub, sub)] = nt(ident_d, block(which, s)).astype(jnp.bfloat16)

        repeat(nsub, one)

    transposed(0)
    rows_out[...] = nn(cd[0], res[...])[:d, :]

    held = None
    for p in peers + [me]:
        rcopy(gcol.at[p], s1buf.at[p // 2], a_s.at[p // 2], a_r.at[p // 2], at_mate).wait_recv()
        if p is me:
            total = gcol[me] + s1buf[mine]
        else:
            s2src[p // 2] = (gcol[p] + s1buf[p // 2]).astype(s2src.dtype)
        if held is not None:
            held.start()
            sends.append(held)
        held = None if p is me else rcopy(
            s2src.at[p // 2], s2buf.at[mine], b_s.at[p // 2], b_r.at[mine], (p, col))

    forward(1)
    mate_blocks(1)
    transposed(1)
    for q in range(nq):
        qs = pl.ds(q * q_w, q_w)
        ecopies[q].wait_recv()

        def cells(s):
            at = pl.ds(s * sub, sub)
            gap = nn(block(1, s), raug[:, qs])
            code = enc[1, q, at, :].astype(jnp.float32)
            slope, logc = slope_terms(code)
            res[at, qs] = cell(code, slope, logc, gap).astype(jnp.bfloat16)

        repeat(nsub, cells)
        rows_out[:, qs] = (rows_out[:, qs] + nn(cd[1], res[:, qs])[:d, :]) * scale_r

    for p in froms:
        rcopy(s2src.at[0], s2buf.at[p // 2], b_s.at[p // 2], b_r.at[p // 2], at_mate).wait_recv()
        total = total + s2buf[p // 2].astype(jnp.float32)
    cols_out[...] = (total * scale_c)[:, :d]
    for cp in sends + ecopies:
        cp.wait_send()


def scratch_bytes(shapes):
    return sum(math.prod(s.shape) * jnp.dtype(s.dtype).itemsize for s in shapes)


def place(rows_in, cols_in, rows_out, cols_out, sem):
    copies = [pltpu.make_async_copy(rows_in, rows_out, sem.at[0]),
              pltpu.make_async_copy(cols_in, cols_out, sem.at[1])]
    for cp in copies:
        cp.start()
    for cp in copies:
        cp.wait()


def body(row_embed, col_embed, counts, occupancy, row_marg, col_marg, log_total):
    n = lax.axis_size("row")
    d, rows = row_embed.shape
    w = col_embed.shape[2]
    band = counts.shape[2]
    tile = rows // occupancy.shape[0]
    q_w = 2 * tile if rows % (2 * tile) == 0 else tile
    dp = -(-(d + 6) // LANES) * LANES
    half = n // 2
    nq = rows // q_w
    btiles = band // LANES
    cfg = (n, d, dp, w, band, rows, tile, q_w,
           1.0 / math.sqrt(w * n * lax.axis_size("col")), 1.0 / math.sqrt(rows * n))
    bf, f32 = jnp.bfloat16, jnp.float32
    vm, hb, anywhere = (pl.BlockSpec(memory_space=m) for m in (pltpu.VMEM, pltpu.HBM, pl.ANY))
    dma = lambda *s: pltpu.SemaphoreType.DMA(s) if s else pltpu.SemaphoreType.DMA
    scratch = [
        pltpu.VMEM((d, rows), bf),
        pltpu.VMEM((rows * btiles, LANES), jnp.int32),
        pltpu.VMEM((dp, rows), bf),
        pltpu.VMEM((w, dp), f32),
        pltpu.VMEM((2, n, w, dp), bf),
        pltpu.VMEM((2, dp, band), bf),
        pltpu.VMEM((2, nq, band, q_w), bf),
        pltpu.VMEM((nq, band, q_w), f32),
        pltpu.VMEM((nq, band, q_w), f32),
        pltpu.VMEM((band, rows), bf),
        pltpu.VMEM((n, w, dp), f32),
        pltpu.VMEM((half, w, dp), f32),
        pltpu.VMEM((half, w, dp), SEND),
        pltpu.VMEM((half, w, dp), SEND),
        pltpu.VMEM((w, d), bf),
        pltpu.VMEM((occupancy.shape[2], occupancy.shape[0]), jnp.int32),
        pltpu.VMEM((1, rows), jnp.int32),
        pltpu.VMEM((1, w), jnp.int32),
        dma(nq + 5),
        dma(2, half), dma(2, half), dma(2, half), dma(2, half), dma(), dma(),
        dma(nq), dma(nq), dma(half), dma(half), dma(half), dma(half),
        pltpu.SemaphoreType.REGULAR((half.bit_length() - 1,)),
    ]
    limit = min(60 << 20, (6 << 20) + scratch_bytes(scratch[:18]) + 2 * d * rows * 4 + 24 * band * q_w)
    grad_rows, grad_cols = pl.pallas_call(
        functools.partial(kernel, cfg),
        out_shape=(jax.ShapeDtypeStruct((d, rows), f32), jax.ShapeDtypeStruct((w, d), f32)),
        in_specs=[hb] * 6 + [pl.BlockSpec(memory_space=pltpu.SMEM)],
        out_specs=(vm, vm),
        scratch_shapes=scratch,
        compiler_params=pltpu.CompilerParams(
            collective_id=0, has_side_effects=True, vmem_limit_bytes=limit),
    )(
        *(pltpu.with_memory_space_constraint(x, pltpu.HBM) for x in (
            row_embed,
            jnp.transpose(col_embed, (1, 2, 0)).reshape(w, d),
            counts.reshape(rows * btiles, LANES),
            jnp.transpose(occupancy, (1, 2, 0)).reshape(occupancy.shape[2], occupancy.shape[0]),
            row_marg.reshape(1, rows),
            col_marg,
        )),
        log_total,
    )
    grad_rows, grad_cols = pl.pallas_call(
        place,
        out_shape=(jax.ShapeDtypeStruct((d, rows), f32), jax.ShapeDtypeStruct((w, d), f32)),
        in_specs=[anywhere, anywhere],
        out_specs=(hb, hb),
        scratch_shapes=[pltpu.SemaphoreType.DMA((2,))],
    )(*(pltpu.with_memory_space_constraint(x, pltpu.VMEM) for x in (grad_rows, grad_cols)))
    return grad_rows, jnp.transpose(grad_cols.reshape(1, w, d), (2, 0, 1))


def solution(mesh):
    placed = (
        P(None, "row"),
        P(None, "col", "row"),
        P("row", "col", None),
        P("row", "col", None),
        P("row"),
        P("col", "row"),
        P(),
    )
    return jax.shard_map(
        body,
        mesh=mesh,
        in_specs=placed,
        out_specs=(P(None, "row"), P(None, "col", "row")),
        check_vma=False,
    )
```
